512 devices in a mesh: row: 64 (over z_lo, y, x), col: 8 (over z_hi, core).
Axes of the slice: x: 4, y: 4, z: 16 (z_hi: 4, z_lo: 4; z = z_hi * 4 + z_lo), core: 2. Of those that a mesh axis runs over, the one named last changes fastest.
Arguments:
- front: float32 [65536, 1024], P('row', 'col'), may hold values from -6 to 6
- contrib: bfloat16 [524288, 1024], P('row', 'col'), may hold values from -6 to 6
- target: int32 [2048], replicated, may hold values from 0 to 255, as said below
- mask: int32 [256, 8], P('row', 'col'), may hold values 0 or 1
- panel: float32 [65536, 256], P(('row', 'col')), as said below
- pivots: int32 [256], replicated, may hold values from 0 to 65535, as said below
Outputs:
- lower: float32 [65536, 256], P(('row', 'col'))
- schur: float32 [65536, 1024], P('row', 'col')
The draws below stay inside these ranges and needn't reach their ends.
Inputs may be any that keep to these rules, and one draw needn't show every extreme that they name: Front block row t lies on index t // 4 of row. Within each aligned block of 32 entries (one device's contribution blocks) the values target // 4 are distinct, and index 0 of row receives a block from every aligned block. `pivots`: distinct rows; each aligned group of 1024 rows holds exactly 4 of them. The 256 x 256 matrix formed by the panel's rows named in pivots is invertible.
All inputs are finite; a program needn't handle non-finite values. No bound on the sum of `mask` on one device may be relied on, other than what follows from the above.
Results may differ from the reference program's by a relative error of at most 0.0003.
Values may be sent and summed in bfloat16 or wider, within the bound.
No kernel may reach another device: no remote copies, remote signals or barrier semaphores. Data moves between devices by JAX's collectives and lax.ppermute only.
A program may use at most 64 MiB of HBM per device.

```python
import jax
import jax.numpy as jnp
from jax import lax

BLK = 256
W = 256
FB_DEV = 4
CC = 128
F = 65536
FBT = 256
C = 1024
CBR = 32
N_ROW = 64
N_COL = 8


def pick_pivots(key):
    base_key = jax.random.fold_in(key, 7)
    order_key, offset_key = jax.random.split(base_key)
    group_rows = FB_DEV * BLK
    per_group = W // N_ROW
    order = jax.random.permutation(order_key, W)
    group_keys = jax.random.split(offset_key, N_ROW)
    offsets = jax.vmap(lambda sub_key: jax.random.permutation(sub_key, group_rows)[:per_group])(group_keys).astype(jnp.int32)
    group_ids = jnp.arange(N_ROW, dtype=jnp.int32)
    forced = jnp.where(group_ids == N_ROW - 1, group_rows - 1, 0)
    shifts = jnp.where((group_ids == 0) | (group_ids == N_ROW - 1), forced - offsets[:, 0], 0)
    offsets = (offsets + shifts[:, None] + group_rows) % group_rows
    starts = group_ids[:, None] * group_rows
    chosen = (starts + offsets).reshape(W)
    result = jnp.zeros((W,), jnp.int32).at[order].set(chosen)
    return result.astype(jnp.int32)


def draw_pivots(key, part):
    return pick_pivots(key)


def draw_panel(key, part):
    pivot_rows = pick_pivots(key)
    key_base, key_diag, key_off = jax.random.split(jax.random.fold_in(key, 11), 3)
    total_rows = FB_DEV * BLK * N_ROW
    values = 0.5 * jax.random.normal(key_base, (total_rows, W))
    flags = jnp.zeros((total_rows,), jnp.int32).at[pivot_rows].set(1)
    columns = jnp.zeros((total_rows,), jnp.int32).at[pivot_rows].set(jnp.arange(W, dtype=jnp.int32))
    spread = 2.0 / (W - 1)
    off_diag = jax.random.uniform(key_off, (total_rows, W), minval=-spread, maxval=spread)
    diagonal = jax.random.uniform(key_diag, (total_rows, 1), minval=3.0, maxval=4.0)
    on_diag = jnp.arange(W, dtype=jnp.int32)[None, :] == columns[:, None]
    dominant = jnp.where(on_diag, diagonal, off_diag)
    return jnp.where(flags[:, None] == 1, dominant, values).astype(jnp.float32)


def draw_target(key, part):
    key_dest, key_block = jax.random.split(jax.random.fold_in(key, 3), 2)
    source_ids = jnp.arange(N_ROW, dtype=jnp.int32)

    def one_source(sub_key, source):
        shuffled = jax.random.permutation(sub_key, N_ROW - 1)[:CBR - 1].astype(jnp.int32)
        shift = jnp.where(source == 0, N_ROW - 2 - shuffled[0], 0)
        shuffled = (shuffled + shift + (N_ROW - 1)) % (N_ROW - 1)
        others = 1 + shuffled
        return jnp.concatenate([jnp.zeros((1,), jnp.int32), others])
    dest_all = jax.vmap(one_source)(jax.random.split(key_dest, N_ROW), source_ids)
    block_in = jax.random.randint(key_block, (N_ROW, CBR), 0, FB_DEV).astype(jnp.int32)
    block_in = block_in.at[0, 0].set(0)
    block_in = block_in.at[0, 1].set(FB_DEV - 1)
    return (dest_all * FB_DEV + block_in).reshape(N_ROW * CBR).astype(jnp.int32)


def with_ends(array, stream_key, smallest, high):
    extent = array.shape
    spot = [jax.random.randint(jax.random.fold_in(stream_key, axis), (), 0, extent[axis]) for axis in range(len(extent))]
    array = array.at[tuple(spot)].set(smallest)
    longest = extent.index(max(extent))
    spot[longest] = (spot[longest] + 1) % extent[longest]
    return array.at[tuple(spot)].set(high)


def levels(own_key, shape, shards, low, high):
    gain, own = 1.0, jax.random.fold_in(own_key, 6)
    for axis_at, parts in shards:
        heights = jnp.exp(jax.random.uniform(jax.random.fold_in(own, axis_at), (parts,), jnp.float32, low / len(shards), high / len(shards)))
        gain = gain * jnp.repeat(heights, shape[axis_at] // parts).reshape([-1 if axis == axis_at else 1 for axis in range(len(shape))])
    return gain


def centred(rng, dims, deviation, bound, cuts=(), kind=jnp.bfloat16):
    entries = jax.random.normal(rng, dims, jnp.float32) * deviation
    if len(cuts) > 0:
        entries = levels(rng, dims, cuts, -0.22, 0.18) * entries
    return jnp.clip(entries, min=-bound, max=bound).astype(kind)


def setup_inputs(seed: int = 0) -> dict:
    key_list = jax.random.split(jax.random.key(seed), 7)
    front = centred(key_list[0], (F, C), 1.0, 6.0, ((0, 64), (1, 8)), jnp.float32)
    contrib = centred(key_list[1], (N_ROW * CBR * BLK, C), 1.0, 6.0, ((0, 64), (1, 8)))
    target = draw_target(jax.random.fold_in(key_list[6], 71), 0)
    mask = with_ends((jax.random.randint(key_list[3], (FBT, N_COL), 0, 4) < 3).astype(jnp.int32), jax.random.fold_in(key_list[3], 1), 0, 1)
    panel = draw_panel(jax.random.fold_in(key_list[6], 71), 0)
    pivots = draw_pivots(jax.random.fold_in(key_list[6], 71), 0)
    return dict(front=front, contrib=contrib, target=target, mask=mask, panel=panel, pivots=pivots)


def reference(front, contrib, target, mask, panel, pivots):
    blocks = contrib.reshape(N_ROW * CBR, BLK, C).astype(jnp.float32)
    summed = jax.ops.segment_sum(blocks, target, num_segments=FBT)
    assembled = front + summed.reshape(F, C)
    pivot_block = panel[pivots]
    lower = jnp.linalg.solve(pivot_block.T, panel.T).T
    upper = assembled[pivots]
    update = jnp.dot(lower, upper, precision=lax.Precision.HIGHEST)
    row_mask = jnp.repeat(mask.astype(jnp.float32), BLK, axis=0)
    full_mask = jnp.repeat(row_mask, CC, axis=1)
    schur = assembled - full_mask * update
    return (lower, schur)
```

```python
import jax
import jax.numpy as jnp
from jax import lax
from jax.sharding import PartitionSpec as P

BLK = 256


def exact_dot(left, right):
    return jnp.dot(left, right, precision=lax.Precision.HIGHEST, preferred_element_type=jnp.float32)


def spread_rows(rows):
    count = lax.axis_size("row")
    sent = jnp.broadcast_to(rows[None], (count,) + rows.shape)
    return lax.all_to_all(sent, "row", split_axis=0, concat_axis=0, tiled=True).reshape(-1, rows.shape[-1])


def sum_over_col(value):
    count = lax.axis_size("col")
    step = 1
    while step < count:
        value = value + lax.ppermute(value, "col", [(c, c ^ step) for c in range(count)])
        step *= 2
    return value


def body(front, contrib, target, mask, panel, pivots):
    row_count = lax.axis_size("row")
    row_index = lax.axis_index("row")
    col_index = lax.axis_index("col")
    tile_rows, tile_cols = front.shape
    blocks_own = tile_rows // BLK
    sent_count = contrib.shape[0] // BLK
    targets = target.reshape(row_count, sent_count)

    width = pivots.shape[0]
    own_count = width // row_count
    rank = jnp.sum((pivots[:, None] > pivots[None, :]).astype(jnp.int32), axis=1)
    order = rank[None, :] == jnp.arange(width, dtype=jnp.int32)[:, None]
    own_slots = row_index * own_count + jnp.arange(own_count, dtype=jnp.int32)
    own_order = rank[None, :] == own_slots[:, None]
    own_pivots = jnp.sum(jnp.where(own_order, pivots[None, :], 0), axis=1) - row_index * tile_rows

    panel_rows = panel.shape[0]
    select_rows = (
        own_pivots[:, None] - col_index * panel_rows == jnp.arange(panel_rows, dtype=jnp.int32)[None, :]
    ).astype(jnp.float32)
    pivot_sorted = sum_over_col(spread_rows(exact_dot(select_rows, panel)))

    own_targets = lax.dynamic_slice_in_dim(targets, row_index, 1, 0)[0]
    device_ids = jnp.arange(row_count, dtype=jnp.int32)
    chooser = (own_targets[None, :] // blocks_own == device_ids[:, None]).astype(jnp.bfloat16)
    pieces = contrib.reshape(sent_count, BLK, tile_cols)
    outgoing = jnp.einsum(
        "db,bxc->dxc", chooser, pieces, preferred_element_type=jnp.float32
    ).astype(jnp.bfloat16)
    arrived = lax.all_to_all(outgoing, "row", split_axis=0, concat_axis=0, tiled=True)
    panel_full = lax.all_gather(panel, "col", axis=0, tiled=True)

    gram = exact_dot(pivot_sorted, pivot_sorted.T)
    factor_low = jnp.linalg.cholesky(gram)
    inverse_sorted = jax.scipy.linalg.cho_solve((factor_low, True), pivot_sorted).T
    lower_own = exact_dot(panel, exact_dot(inverse_sorted, order.astype(jnp.float32)))

    block_ids = jnp.arange(blocks_own, dtype=jnp.int32)
    own_blocks = row_index * blocks_own + block_ids
    placing = jnp.sum(
        (targets[:, :, None] == own_blocks[None, None, :]).astype(jnp.float32), axis=1
    ).astype(jnp.bfloat16)
    added = jnp.einsum("sk,sxc->kxc", placing, arrived, preferred_element_type=jnp.float32).reshape(
        tile_rows, tile_cols
    )
    assembled = front + added
    picker = (own_pivots[:, None] == jnp.arange(tile_rows, dtype=jnp.int32)[None, :]).astype(jnp.float32)
    upper_sorted = spread_rows(exact_dot(picker, assembled))
    update = exact_dot(panel_full, exact_dot(inverse_sorted, upper_sorted))
    row_mask = jnp.repeat(mask[:, 0].astype(jnp.float32), BLK)
    schur = assembled - row_mask[:, None] * update
    return (lower_own, schur)


def solution(mesh):
    placed = (P("row", "col"), P("row", "col"), P(), P("row", "col"), P(("row", "col"), None), P())
    return jax.shard_map(
        body,
        mesh=mesh,
        in_specs=placed,
        out_specs=(P(("row", "col"), None), P("row", "col")),
        check_vma=False,
    )
```

```python
import functools

import jax
import jax.numpy as jnp
from jax import lax
from jax.experimental import pallas as pl
from jax.experimental.pallas import tpu as pltpu
from jax.sharding import PartitionSpec as P

BLK = 256
PLANE = 16
LAYERS = 4
PICK = 4


def exact_dot(left, right):
    return jnp.dot(left, right, precision=lax.Precision.HIGHEST, preferred_element_type=jnp.float32)


def pack_kernel(count, tgt_ref, contrib_ref, out_ref, sems):
    here = lax.axis_index("row")

    def copy(b):
        dest = tgt_ref[here * count + b] // LAYERS
        away = (dest // PLANE) ^ (here // PLANE)
        return pltpu.make_async_copy(contrib_ref.at[b], out_ref.at[dest % PLANE, away], sems.at[b])

    for b in range(count):
        copy(b).start()
    for b in range(count):
        copy(b).wait()


def pack(target, pieces):
    count, rows, cols = pieces.shape
    return pl.pallas_call(
        functools.partial(pack_kernel, count),
        out_shape=jax.ShapeDtypeStruct((PLANE, LAYERS, rows, cols), pieces.dtype),
        grid_spec=pltpu.PrefetchScalarGridSpec(
            num_scalar_prefetch=1,
            grid=(),
            in_specs=[pl.BlockSpec(memory_space=pltpu.VMEM)],
            out_specs=pl.BlockSpec(memory_space=pl.ANY),
            scratch_shapes=[pltpu.SemaphoreType.DMA((count,))],
        ),
        compiler_params=pltpu.CompilerParams(vmem_limit_bytes=48 << 20),
        cost_estimate=pl.CostEstimate(flops=0, bytes_accessed=4 << 20, transcendentals=0),
        name="pack",
    )(target, pieces)


def fold_kernel(kind_ref, off_ref, spot_ref, arrived_ref, front_ref, mine_ref, other_ref, *outs):
    sums, row_ref, upper_ref = outs[:LAYERS], outs[LAYERS], outs[LAYERS + 1]
    lanes = arrived_ref.shape[3]
    layer = lax.axis_index("row") // PLANE
    for away, out in enumerate(sums):
        out[...] = jnp.zeros_like(out)
        for s in range(PLANE):
            kind = kind_ref[s * LAYERS + away]

            @pl.when(kind >= 0)
            def _():
                spot = pl.ds(pl.multiple_of(jnp.maximum(kind, 0) * BLK, BLK), BLK)
                out[spot, :] = out[spot, :] + arrived_ref[s, away].astype(jnp.float32)

        for i in range(PICK):
            picked = out[pl.ds(off_ref[away * PICK + i], 1), :]
            if away == 0:
                picked = picked + front_ref[i : i + 1, :]
            upper_ref[pl.ds((layer ^ away) * PICK + i, 1), :] = picked
    row_ref[:, :lanes] = upper_ref[...]
    half, width = mine_ref.shape
    line = lax.broadcasted_iota(jnp.int32, (row_ref.shape[0], width), 0)
    inside = lax.broadcasted_iota(jnp.int32, (8, width), 0)
    pivot_rows = jnp.zeros((row_ref.shape[0], width), jnp.float32)
    for i in range(PICK):
        spot = spot_ref[i]
        tile = pl.ds(pl.multiple_of(spot % half // 8 * 8, 8), 8)
        rows = jnp.where(spot < half, mine_ref[tile, :], other_ref[tile, :])
        row = jnp.sum(jnp.where(inside == spot % 8, rows, 0.0), axis=0, keepdims=True)
        pivot_rows = pivot_rows + jnp.where(line == layer * PICK + i, row, 0.0)
    row_ref[:, lanes:] = pivot_rows


def fold(kinds, offsets, spots, arrived, front_picked, mine, other):
    _, _, rows, cols = arrived.shape
    whole = jax.ShapeDtypeStruct((LAYERS * rows, cols), jnp.float32)
    vmem = pl.BlockSpec(memory_space=pltpu.VMEM)
    return pl.pallas_call(
        fold_kernel,
        out_shape=(whole,) * LAYERS
        + (jax.ShapeDtypeStruct((LAYERS * PICK, cols + mine.shape[1]), jnp.float32),),
        grid_spec=pltpu.PrefetchScalarGridSpec(
            num_scalar_prefetch=3, grid=(), in_specs=[vmem] * 4, out_specs=(vmem,) * (LAYERS + 1),
            scratch_shapes=[pltpu.VMEM((LAYERS * PICK, cols), jnp.float32)],
        ),
        compiler_params=pltpu.CompilerParams(vmem_limit_bytes=24 << 20),
        cost_estimate=pl.CostEstimate(flops=4 << 20, bytes_accessed=7 << 20, transcendentals=0),
        name="fold",
    )(kinds, offsets, spots, arrived, front_picked, mine, other)


def finish_kernel(mask_ref, got_ref, place_ref, mine_ref, other_ref, front_ref, near_ref, lower_ref, kept_ref, a_ref, x_ref):
    n, lanes = a_ref.shape[0], front_ref.shape[1]
    given = got_ref[:, :, lanes:].reshape(n, n)
    turned = given.T
    a = given * (1.0 / jnp.max(jnp.abs(given), axis=1, keepdims=True))
    scale = 1.0 / jnp.max(jnp.abs(turned), axis=0, keepdims=True)
    size = jnp.max(jnp.sum(jnp.abs(a), axis=1)) * jnp.max(jnp.sum(jnp.abs(a), axis=0))
    a_ref[...] = a
    x_ref[...] = turned * scale * (1.0 / size)
    rows = lax.broadcasted_iota(jnp.int32, (n, n), 0)
    eye = (rows == lax.broadcasted_iota(jnp.int32, (n, n), 1)).astype(jnp.float32)

    def going(state):
        step, now, before = state
        stalled = (now < 0.01) & (now > 0.25 * before)
        return (step < 90) & (now > 4e-8) & jnp.logical_not(stalled)

    def improve(state):
        step, now, _ = state
        x = x_ref[...]
        residual = eye - exact_dot(a_ref[...], x)
        x_ref[...] = x + exact_dot(x, residual)
        return step + 1, jnp.sum(residual * residual), now

    lax.while_loop(going, improve, (jnp.int32(0), jnp.float32(1e6), jnp.float32(1e12)))
    inverse = x_ref[...] * scale
    solved = exact_dot(inverse, got_ref[:, :, :lanes].reshape(n, lanes))
    here = lax.axis_index("col")
    part = lower_ref.shape[0]
    around = mine_ref.shape[0] // part
    for across, panel_ref in enumerate((mine_ref, other_ref)):
        for turn in range(around):
            update = exact_dot(panel_ref[turn * part : (turn + 1) * part, :], solved)
            owner = (here // 2 + turn) % around * 2 + (here % 2 + across) % 2
            spot = pl.ds(pl.multiple_of(owner * part, part), part)
            keep = mask_ref[owner * part // BLK].astype(jnp.float32)
            kept_ref[spot, :] = front_ref[spot, :] + near_ref[spot, :] - keep * update
    order = (rows == place_ref[...]).astype(jnp.float32)
    lower_ref[...] = exact_dot(mine_ref[:part, :], exact_dot(inverse, order))


def finish(mask, got, place, mine, other, front, near, part):
    n = place.shape[0]
    vmem = pl.BlockSpec(memory_space=pltpu.VMEM)
    return pl.pallas_call(
        finish_kernel,
        out_shape=(jax.ShapeDtypeStruct((part, n), jnp.float32), jax.ShapeDtypeStruct(front.shape, jnp.float32)),
        grid_spec=pltpu.PrefetchScalarGridSpec(
            num_scalar_prefetch=1,
            grid=(),
            in_specs=[vmem] * 6,
            out_specs=(vmem, vmem),
            scratch_shapes=[pltpu.VMEM((n, n), jnp.float32), pltpu.VMEM((n, n), jnp.float32)],
        ),
        compiler_params=pltpu.CompilerParams(vmem_limit_bytes=24 << 20),
        cost_estimate=pl.CostEstimate(flops=0, bytes_accessed=0, transcendentals=0),
        name="finish",
    )(mask, got, place.reshape(1, n), mine, other, front, near)


def share_panel(panel):
    count = lax.axis_size("col")
    around = count // 2
    half = panel.shape[0] // 2

    def turn(value, by):
        return lax.ppermute(value, "col", [(c, (c // 2 + by) % around * 2 + c % 2) for c in range(count)])

    before, after = turn(panel, 1), turn(panel, -1)
    far_low, far_high = turn(before[:half], 1), turn(after[half:], -1)
    mine = jnp.concatenate([panel, after, far_low, far_high, before])
    return mine, lax.ppermute(mine, "col", [(c, c ^ 1) for c in range(count)])


def body(front, contrib, target, mask, panel, pivots):
    row_count = lax.axis_size("row")
    col_count = lax.axis_size("col")
    row_index = lax.axis_index("row")
    col_index = lax.axis_index("col")
    layer = row_index // PLANE
    tile_rows, tile_cols = front.shape
    blocks_own = tile_rows // BLK
    sent_count = contrib.shape[0] // BLK
    width = pivots.shape[0]
    planes = [[z * PLANE + i for i in range(PLANE)] for z in range(LAYERS)]

    def over_plane(value):
        return lax.all_to_all(
            value, "row", split_axis=0, concat_axis=0, axis_index_groups=planes, tiled=True
        )

    def along_z(value, away):
        return lax.ppermute(value, "row", [(r, r ^ (away * PLANE)) for r in range(row_count)])

    rank = jnp.sum((pivots[:, None] > pivots[None, :]).astype(jnp.int32), axis=1)
    groups = row_index ^ (jnp.arange(LAYERS, dtype=jnp.int32) * PLANE)
    slots = (groups[:, None] * PICK + jnp.arange(PICK, dtype=jnp.int32)[None, :]).reshape(-1)
    chosen = jnp.sum(jnp.where(rank[None, :] == slots[:, None], pivots[None, :], 0), axis=1)
    offsets = chosen - jnp.repeat(groups, PICK) * tile_rows

    plane_targets = lax.dynamic_slice_in_dim(target.reshape(row_count, sent_count), layer * PLANE, PLANE, 0)
    hit = (plane_targets // blocks_own)[:, None, :] == groups[None, :, None]
    kinds = jnp.sum(jnp.where(hit, (plane_targets % blocks_own + 1)[:, None, :], 0), axis=2).reshape(-1) - 1

    arrived = over_plane(pack(target, contrib.reshape(sent_count, BLK, tile_cols)))
    panel_rows = panel.shape[0]
    mine, other = share_panel(panel)
    owner, around = offsets[:PICK] // panel_rows, col_count // 2
    turns = (owner // 2 - col_index // 2) % around
    across = (owner + col_index) % 2
    spots = (across * around + turns) * panel_rows + offsets[:PICK] % panel_rows
    picker = (offsets[:PICK, None] == jnp.arange(tile_rows, dtype=jnp.int32)[None, :]).astype(jnp.float32)
    front_picked = exact_dot(picker, front)
    place = (rank // PICK) % PLANE * (LAYERS * PICK) + rank // (PICK * PLANE) * PICK + rank % PICK
    arrived, place = lax.optimization_barrier((arrived, place))

    near0, near1, far2, far3, lines = fold(kinds, offsets, spots, arrived, front_picked, mine, other)
    lines = lines + along_z(lines, 1) + along_z(lines, 2) + along_z(lines, 3)
    lines, near1, far2, far3 = lax.optimization_barrier((lines, near1, far2, far3))
    got1, got2, got3 = along_z(near1, 1), along_z(far2, 2), along_z(far3, 3)
    got = over_plane(jnp.broadcast_to(lines[None], (PLANE,) + lines.shape))
    lower_own, kept = finish(mask.reshape(-1), got, place, mine, other, front, near0, panel_rows)
    return (lower_own, kept + got1 + (got2 + got3))


def solution(mesh):
    placed = (P("row", "col"), P("row", "col"), P(), P("row", "col"), P(("row", "col"), None), P())
    return jax.shard_map(
        body,
        mesh=mesh,
        in_specs=placed,
        out_specs=(P(("row", "col"), None), P("row", "col")),
        check_vma=False,
    )
```

```python
import functools

import jax
import jax.numpy as jnp
from jax import lax
from jax.experimental import pallas as pl
from jax.experimental.pallas import tpu as pltpu
from jax.sharding import PartitionSpec as P

BLK = 256
PLANE = 16
LAYERS = 4
PICK = 4


def exact_dot(left, right):
    return jnp.dot(left, right, precision=lax.Precision.HIGHEST, preferred_element_type=jnp.float32)


def pack_kernel(count, tgt_ref, contrib_ref, out_ref, held_ref, sems):
    here = lax.axis_index("row")

    def bring(b):
        return pltpu.make_async_copy(contrib_ref.at[b], held_ref.at[b], sems.at[0, b])

    def send(b):
        dest = tgt_ref[here * count + b] >> 2
        away = (dest >> 4) ^ (here >> 4)
        return pltpu.make_async_copy(held_ref.at[b], out_ref.at[dest & (PLANE - 1), away], sems.at[1, b])

    for b in range(count):
        bring(b).start()
    for b in range(count):
        bring(b).wait()
        send(b).start()
    for b in range(count):
        send(b).wait()


def pack(target, pieces):
    count, rows, cols = pieces.shape
    return pl.pallas_call(
        functools.partial(pack_kernel, count),
        out_shape=jax.ShapeDtypeStruct((PLANE, LAYERS, rows, cols), pieces.dtype),
        grid_spec=pltpu.PrefetchScalarGridSpec(
            num_scalar_prefetch=1,
            grid=(),
            in_specs=[pl.BlockSpec(memory_space=pltpu.HBM)],
            out_specs=pl.BlockSpec(memory_space=pltpu.HBM),
            scratch_shapes=[
                pltpu.VMEM((count, rows, cols), pieces.dtype),
                pltpu.SemaphoreType.DMA((2, count)),
            ],
        ),
        compiler_params=pltpu.CompilerParams(vmem_limit_bytes=60 << 20),
        cost_estimate=pl.CostEstimate(flops=0, bytes_accessed=4 << 20, transcendentals=0),
        name="pack",
    )(target, pieces)


def fold_kernel(kind_ref, off_ref, spot_ref, arrived_ref, front_ref, mine_ref, other_ref, *outs):
    sums, row_ref, upper_ref = outs[:LAYERS], outs[LAYERS], outs[LAYERS + 1]
    lanes = arrived_ref.shape[3]
    layer = lax.axis_index("row") // PLANE
    for away, out in enumerate(sums):
        out[...] = jnp.zeros_like(out)
        for s in range(PLANE):
            kind = kind_ref[s * LAYERS + away]

            @pl.when(kind >= 0)
            def _():
                spot = pl.ds(pl.multiple_of(jnp.maximum(kind, 0) * BLK, BLK), BLK)
                out[spot, :] = out[spot, :] + arrived_ref[s, away].astype(jnp.float32)

        for i in range(PICK):
            picked = out[pl.ds(off_ref[away * PICK + i], 1), :]
            if away == 0:
                picked = picked + front_ref[i : i + 1, :]
            upper_ref[pl.ds((layer ^ away) * PICK + i, 1), :] = picked
    row_ref[:, :lanes] = upper_ref[...]
    half, width = mine_ref.shape
    line = lax.broadcasted_iota(jnp.int32, (row_ref.shape[0], width), 0)
    inside = lax.broadcasted_iota(jnp.int32, (8, width), 0)
    pivot_rows = jnp.zeros((row_ref.shape[0], width), jnp.float32)
    for i in range(PICK):
        spot = spot_ref[i]
        tile = pl.ds(pl.multiple_of(spot % half // 8 * 8, 8), 8)
        rows = jnp.where(spot < half, mine_ref[tile, :], other_ref[tile, :])
        row = jnp.sum(jnp.where(inside == spot % 8, rows, 0.0), axis=0, keepdims=True)
        pivot_rows = pivot_rows + jnp.where(line == layer * PICK + i, row, 0.0)
    row_ref[:, lanes:] = pivot_rows


def fold(kinds, offsets, spots, arrived, front_picked, mine, other):
    _, _, rows, cols = arrived.shape
    whole = jax.ShapeDtypeStruct((LAYERS * rows, cols), jnp.float32)
    vmem = pl.BlockSpec(memory_space=pltpu.VMEM)
    return pl.pallas_call(
        fold_kernel,
        out_shape=(whole,) * LAYERS
        + (jax.ShapeDtypeStruct((LAYERS * PICK, cols + mine.shape[1]), jnp.float32),),
        grid_spec=pltpu.PrefetchScalarGridSpec(
            num_scalar_prefetch=3, grid=(), in_specs=[vmem] * 4, out_specs=(vmem,) * (LAYERS + 1),
            scratch_shapes=[pltpu.VMEM((LAYERS * PICK, cols), jnp.float32)],
        ),
        compiler_params=pltpu.CompilerParams(vmem_limit_bytes=24 << 20),
        cost_estimate=pl.CostEstimate(flops=4 << 20, bytes_accessed=7 << 20, transcendentals=0),
        name="fold",
    )(kinds, offsets, spots, arrived, front_picked, mine, other)


def finish_kernel(mask_ref, got_ref, place_ref, mine_ref, other_ref, front_ref, near_ref, lower_ref, kept_ref, a_ref, x_ref):
    n, lanes = a_ref.shape[0], front_ref.shape[1]
    given = got_ref[:, :, lanes:].reshape(n, n)
    turned = given.T
    a = given * (1.0 / jnp.max(jnp.abs(given), axis=1, keepdims=True))
    scale = 1.0 / jnp.max(jnp.abs(turned), axis=0, keepdims=True)
    size = jnp.max(jnp.sum(jnp.abs(a), axis=1)) * jnp.max(jnp.sum(jnp.abs(a), axis=0))
    a_ref[...] = a
    x_ref[...] = turned * scale * (1.0 / size)
    rows = lax.broadcasted_iota(jnp.int32, (n, n), 0)
    eye = (rows == lax.broadcasted_iota(jnp.int32, (n, n), 1)).astype(jnp.float32)

    def going(state):
        step, now, before = state
        stalled = (now < 0.01) & (now > 0.25 * before)
        return (step < 90) & (now > 4e-8) & jnp.logical_not(stalled)

    def improve(state):
        step, now, _ = state
        x = x_ref[...]
        residual = eye - exact_dot(a_ref[...], x)
        x_ref[...] = x + exact_dot(x, residual)
        return step + 1, jnp.sum(residual * residual), now

    lax.while_loop(going, improve, (jnp.int32(0), jnp.float32(1e6), jnp.float32(1e12)))
    inverse = x_ref[...] * scale
    solved = exact_dot(inverse, got_ref[:, :, :lanes].reshape(n, lanes))
    here = lax.axis_index("col")
    part = lower_ref.shape[0]
    around = mine_ref.shape[0] // part
    for across, panel_ref in enumerate((mine_ref, other_ref)):
        for turn in range(around):
            update = exact_dot(panel_ref[turn * part : (turn + 1) * part, :], solved)
            owner = (here // 2 + turn) % around * 2 + (here % 2 + across) % 2
            spot = pl.ds(pl.multiple_of(owner * part, part), part)
            keep = mask_ref[owner * part // BLK].astype(jnp.float32)
            kept_ref[spot, :] = front_ref[spot, :] + near_ref[spot, :] - keep * update
    order = (rows == place_ref[...]).astype(jnp.float32)
    lower_ref[...] = exact_dot(mine_ref[:part, :], exact_dot(inverse, order))


def finish(mask, got, place, mine, other, front, near, part):
    n = place.shape[0]
    vmem = pl.BlockSpec(memory_space=pltpu.VMEM)
    return pl.pallas_call(
        finish_kernel,
        out_shape=(jax.ShapeDtypeStruct((part, n), jnp.float32), jax.ShapeDtypeStruct(front.shape, jnp.float32)),
        grid_spec=pltpu.PrefetchScalarGridSpec(
            num_scalar_prefetch=1,
            grid=(),
            in_specs=[vmem] * 6,
            out_specs=(vmem, vmem),
            scratch_shapes=[pltpu.VMEM((n, n), jnp.float32), pltpu.VMEM((n, n), jnp.float32)],
        ),
        compiler_params=pltpu.CompilerParams(vmem_limit_bytes=24 << 20),
        cost_estimate=pl.CostEstimate(flops=0, bytes_accessed=0, transcendentals=0),
        name="finish",
    )(mask, got, place.reshape(1, n), mine, other, front, near)


def share_panel(panel):
    count = lax.axis_size("col")
    around = count // 2
    half = panel.shape[0] // 2

    def turn(value, by):
        return lax.ppermute(value, "col", [(c, (c // 2 + by) % around * 2 + c % 2) for c in range(count)])

    before, after = turn(panel, 1), turn(panel, -1)
    far_low, far_high = turn(before[:half], 1), turn(after[half:], -1)
    mine = jnp.concatenate([panel, after, far_low, far_high, before])
    return mine, lax.ppermute(mine, "col", [(c, c ^ 1) for c in range(count)])


def body(front, contrib, target, mask, panel, pivots):
    row_count = lax.axis_size("row")
    col_count = lax.axis_size("col")
    row_index = lax.axis_index("row")
    col_index = lax.axis_index("col")
    layer = row_index // PLANE
    tile_rows, tile_cols = front.shape
    blocks_own = tile_rows // BLK
    sent_count = contrib.shape[0] // BLK
    width = pivots.shape[0]
    planes = [[z * PLANE + i for i in range(PLANE)] for z in range(LAYERS)]

    pillars = [[z * PLANE + i for z in range(LAYERS)] for i in range(PLANE)]

    def exchange(value, groups_of):
        return lax.all_to_all(
            value, "row", split_axis=0, concat_axis=0, axis_index_groups=groups_of, tiled=True
        )

    def over_plane(value):
        return exchange(value, planes)

    def over_z(value):
        return exchange(value, pillars)

    def along_z(value, away):
        return lax.ppermute(value, "row", [(r, r ^ (away * PLANE)) for r in range(row_count)])

    rank = jnp.sum((pivots[:, None] > pivots[None, :]).astype(jnp.int32), axis=1)
    groups = row_index ^ (jnp.arange(LAYERS, dtype=jnp.int32) * PLANE)
    slots = (groups[:, None] * PICK + jnp.arange(PICK, dtype=jnp.int32)[None, :]).reshape(-1)
    chosen = jnp.sum(jnp.where(rank[None, :] == slots[:, None], pivots[None, :], 0), axis=1)
    offsets = chosen - jnp.repeat(groups, PICK) * tile_rows

    plane_targets = lax.dynamic_slice_in_dim(target.reshape(row_count, sent_count), layer * PLANE, PLANE, 0)
    hit = (plane_targets // blocks_own)[:, None, :] == groups[None, :, None]
    kinds = jnp.sum(jnp.where(hit, (plane_targets % blocks_own + 1)[:, None, :], 0), axis=2).reshape(-1) - 1

    arrived = over_plane(pack(target, contrib.reshape(sent_count, BLK, tile_cols)))
    panel_rows = panel.shape[0]
    mine, other = share_panel(panel)
    owner, around = offsets[:PICK] // panel_rows, col_count // 2
    turns = (owner // 2 - col_index // 2) % around
    across = (owner + col_index) % 2
    spots = (across * around + turns) * panel_rows + offsets[:PICK] % panel_rows
    picker = (offsets[:PICK, None] == jnp.arange(tile_rows, dtype=jnp.int32)[None, :]).astype(jnp.float32)
    front_picked = exact_dot(picker, front)
    place = (rank // PICK) % PLANE * (LAYERS * PICK) + rank // (PICK * PLANE) * PICK + rank % PICK
    arrived, place = lax.optimization_barrier((arrived, place))

    near0, near1, far2, far3, lines = fold(kinds, offsets, spots, arrived, front_picked, mine, other)
    lines = jnp.sum(over_z(jnp.broadcast_to(lines[None], (LAYERS,) + lines.shape)), axis=0)
    lines, near1, far2, far3 = lax.optimization_barrier((lines, near1, far2, far3))
    got1, got2, got3 = along_z(near1, 1), along_z(far2, 2), along_z(far3, 3)
    got = over_plane(jnp.broadcast_to(lines[None], (PLANE,) + lines.shape))
    lower_own, kept = finish(mask.reshape(-1), got, place, mine, other, front, near0, panel_rows)
    return (lower_own, kept + got1 + (got2 + got3))


def solution(mesh):
    placed = (P("row", "col"), P("row", "col"), P(), P("row", "col"), P(("row", "col"), None), P())
    return jax.shard_map(
        body,
        mesh=mesh,
        in_specs=placed,
        out_specs=(P(("row", "col"), None), P("row", "col")),
        check_vma=False,
    )
```

```python
import functools

import jax
import jax.numpy as jnp
from jax import lax
from jax.experimental import pallas as pl
from jax.experimental.pallas import tpu as pltpu
from jax.sharding import PartitionSpec as P

BLK = 256
PLANE = 16
LAYERS = 4
PICK = 4
TOP = 8388600.0


def exact_dot(left, right):
    return jnp.dot(left, right, precision=lax.Precision.HIGHEST, preferred_element_type=jnp.float32)


def pack_kernel(count, tgt_ref, contrib_ref, out_ref, held_ref, sems):
    here = lax.axis_index("row")

    def bring(b):
        return pltpu.make_async_copy(contrib_ref.at[b], held_ref.at[b], sems.at[0, b])

    def send(b):
        dest = tgt_ref[here * count + b] >> 2
        away = (dest >> 4) ^ (here >> 4)
        return pltpu.make_async_copy(held_ref.at[b], out_ref.at[dest & (PLANE - 1), away], sems.at[1, b])

    for b in range(count):
        bring(b).start()
    for b in range(count):
        bring(b).wait()
        send(b).start()
    for b in range(count):
        send(b).wait()


def pack(target, pieces):
    count, rows, cols = pieces.shape
    return pl.pallas_call(
        functools.partial(pack_kernel, count),
        out_shape=jax.ShapeDtypeStruct((PLANE, LAYERS, rows, cols), pieces.dtype),
        grid_spec=pltpu.PrefetchScalarGridSpec(
            num_scalar_prefetch=1,
            grid=(),
            in_specs=[pl.BlockSpec(memory_space=pltpu.HBM)],
            out_specs=pl.BlockSpec(memory_space=pltpu.HBM),
            scratch_shapes=[
                pltpu.VMEM((count, rows, cols), pieces.dtype),
                pltpu.SemaphoreType.DMA((2, count)),
            ],
        ),
        compiler_params=pltpu.CompilerParams(vmem_limit_bytes=60 << 20),
        cost_estimate=pl.CostEstimate(flops=0, bytes_accessed=4 << 20, transcendentals=0),
        name="pack",
    )(target, pieces)


def encode(total, code, scale):
    rows = total.shape[0]
    step = 64

    def whole(start):
        return jnp.floor(total[start : start + step, :] * scale + 0.5).astype(jnp.int32)

    for start in range(0, rows // 2, step):
        first, second = whole(start), whole(start + rows // 2)
        code[start : start + step, :] = (first >> 8).astype(jnp.int16)
        code[start + rows // 2 : start + rows // 2 + step, :] = (second >> 8).astype(jnp.int16)
        both = (first & 255) + ((second & 255) << 8) - 32768
        code[rows + start : rows + start + step, :] = both.astype(jnp.int16)


def decode_kernel(kept_ref, unit_ref, code1_ref, code2_ref, code3_ref, out_ref):
    layer = lax.axis_index("row") // PLANE
    rows = out_ref.shape[0]
    step = 64
    for start in range(0, rows // 2, step):
        first, second = 0.0, 0.0
        for k, code in enumerate((code1_ref, code2_ref, code3_ref)):
            both = code[rows + start : rows + start + step, :].astype(jnp.int32) + 32768
            spot = unit_ref.shape[1] - 8 + k + 1
            unit = unit_ref[layer ^ (k + 1), spot : spot + 1, : out_ref.shape[1]]
            upper = code[start : start + step, :].astype(jnp.int32)
            first = first + ((upper << 8) + (both & 255)).astype(jnp.float32) * unit
            upper = code[start + rows // 2 : start + rows // 2 + step, :].astype(jnp.int32)
            second = second + ((upper << 8) + (both >> 8)).astype(jnp.float32) * unit
        here = slice(start, start + step)
        out_ref[here, :] = kept_ref[here, :] + first
        here = slice(start + rows // 2, start + rows // 2 + step)
        out_ref[here, :] = kept_ref[here, :] + second


def decode(kept, spread, codes):
    vmem = pl.BlockSpec(memory_space=pltpu.VMEM)
    return pl.pallas_call(
        decode_kernel,
        out_shape=jax.ShapeDtypeStruct(kept.shape, jnp.float32),
        in_specs=[vmem] * 5,
        out_specs=vmem,
        compiler_params=pltpu.CompilerParams(vmem_limit_bytes=16 << 20),
        cost_estimate=pl.CostEstimate(flops=0, bytes_accessed=0, transcendentals=0),
        name="decode",
    )(kept, spread, *codes)


def fold_kernel(kind_ref, off_ref, spot_ref, arrived_ref, front_ref, mine_ref, other_ref, *outs):
    near_ref, codes, row_ref, upper_ref, sum_ref = outs[0], outs[1:LAYERS], outs[-3], outs[-2], outs[-1]
    sums = (near_ref,) + tuple(sum_ref.at[k] for k in range(LAYERS - 1))
    lanes = arrived_ref.shape[3]
    layer = lax.axis_index("row") // PLANE
    for away, out in enumerate(sums):
        out[...] = jnp.zeros_like(out)
        for s in range(PLANE):
            kind = kind_ref[s * LAYERS + away]

            @pl.when(kind >= 0)
            def _():
                spot = pl.ds(pl.multiple_of(jnp.maximum(kind, 0) * BLK, BLK), BLK)
                out[spot, :] = out[spot, :] + arrived_ref[s, away].astype(jnp.float32)

        for i in range(PICK):
            picked = out[pl.ds(off_ref[away * PICK + i], 1), :]
            if away == 0:
                picked = picked + front_ref[i : i + 1, :]
            upper_ref[pl.ds((layer ^ away) * PICK + i, 1), :] = picked
    upper_rows = upper_ref.shape[0]
    row_ref[:upper_rows, :lanes] = upper_ref[...]
    row_ref[upper_rows:, :] = jnp.zeros((row_ref.shape[0] - upper_rows, row_ref.shape[1]), jnp.float32)
    for away in range(1, LAYERS):
        total, code = sums[away], codes[away - 1]
        peak = jnp.maximum(jnp.max(jnp.abs(total[...])), 1e-20)
        row_ref[upper_rows + away : upper_rows + away + 1, :] = jnp.full(
            (1, row_ref.shape[1]), peak * (1.0 / TOP), jnp.float32
        )
        encode(total, code, TOP / peak)
    half, width = mine_ref.shape
    line = lax.broadcasted_iota(jnp.int32, (upper_rows, width), 0)
    inside = lax.broadcasted_iota(jnp.int32, (8, width), 0)
    pivot_rows = jnp.zeros((upper_rows, width), jnp.float32)
    for i in range(PICK):
        spot = spot_ref[i]
        tile = pl.ds(pl.multiple_of(spot % half // 8 * 8, 8), 8)
        rows = jnp.where(spot < half, mine_ref[tile, :], other_ref[tile, :])
        row = jnp.sum(jnp.where(inside == spot % 8, rows, 0.0), axis=0, keepdims=True)
        pivot_rows = pivot_rows + jnp.where(line == layer * PICK + i, row, 0.0)
    row_ref[:upper_rows, lanes:] = pivot_rows


def fold(kinds, offsets, spots, arrived, front_picked, mine, other):
    _, _, rows, cols = arrived.shape
    whole = jax.ShapeDtypeStruct((LAYERS * rows, cols), jnp.float32)
    vmem = pl.BlockSpec(memory_space=pltpu.VMEM)
    return pl.pallas_call(
        fold_kernel,
        out_shape=(whole,)
        + (jax.ShapeDtypeStruct((LAYERS * rows * 3 // 2, cols), jnp.int16),) * (LAYERS - 1)
        + (jax.ShapeDtypeStruct((LAYERS * PICK + 8, cols + mine.shape[1]), jnp.float32),),
        grid_spec=pltpu.PrefetchScalarGridSpec(
            num_scalar_prefetch=3,
            grid=(),
            in_specs=[vmem] * 4,
            out_specs=(vmem,) * (LAYERS + 1),
            scratch_shapes=[
                pltpu.VMEM((LAYERS * PICK, cols), jnp.float32),
                pltpu.VMEM((LAYERS - 1, LAYERS * rows, cols), jnp.float32),
            ],
        ),
        compiler_params=pltpu.CompilerParams(vmem_limit_bytes=24 << 20),
        cost_estimate=pl.CostEstimate(flops=4 << 20, bytes_accessed=7 << 20, transcendentals=0),
        name="fold",
    )(kinds, offsets, spots, arrived, front_picked, mine, other)


def finish_kernel(mask_ref, got_ref, place_ref, mine_ref, other_ref, front_ref, near_ref, lower_ref, kept_ref, a_ref, x_ref):
    n, lanes = a_ref.shape[0], front_ref.shape[1]
    given = got_ref[:, :, lanes:].reshape(n, n)
    turned = given.T
    a = given * (1.0 / jnp.max(jnp.abs(given), axis=1, keepdims=True))
    scale = 1.0 / jnp.max(jnp.abs(turned), axis=0, keepdims=True)
    size = jnp.max(jnp.sum(jnp.abs(a), axis=1)) * jnp.max(jnp.sum(jnp.abs(a), axis=0))
    a_ref[...] = a
    x_ref[...] = turned * scale * (1.0 / size)
    rows = lax.broadcasted_iota(jnp.int32, (n, n), 0)
    eye = (rows == lax.broadcasted_iota(jnp.int32, (n, n), 1)).astype(jnp.float32)

    def going(state):
        step, now, before = state
        stalled = (now < 0.01) & (now > 0.25 * before)
        return (step < 90) & (now > 4e-8) & jnp.logical_not(stalled)

    def improve(state):
        step, now, _ = state
        x = x_ref[...]
        residual = eye - exact_dot(a_ref[...], x)
        x_ref[...] = x + exact_dot(x, residual)
        return step + 1, jnp.sum(residual * residual), now

    lax.while_loop(going, improve, (jnp.int32(0), jnp.float32(1e6), jnp.float32(1e12)))
    inverse = x_ref[...] * scale
    solved = exact_dot(inverse, got_ref[:, :, :lanes].reshape(n, lanes))
    here = lax.axis_index("col")
    part = lower_ref.shape[0]
    around = mine_ref.shape[0] // part
    for across, panel_ref in enumerate((mine_ref, other_ref)):
        for turn in range(around):
            update = exact_dot(panel_ref[turn * part : (turn + 1) * part, :], solved)
            owner = (here // 2 + turn) % around * 2 + (here % 2 + across) % 2
            spot = pl.ds(pl.multiple_of(owner * part, part), part)
            keep = mask_ref[owner * part // BLK].astype(jnp.float32)
            kept_ref[spot, :] = front_ref[spot, :] + near_ref[spot, :] - keep * update
    order = (rows == place_ref[...]).astype(jnp.float32)
    lower_ref[...] = exact_dot(mine_ref[:part, :], exact_dot(inverse, order))


def finish(mask, got, place, mine, other, front, near, part):
    n = place.shape[0]
    vmem = pl.BlockSpec(memory_space=pltpu.VMEM)
    return pl.pallas_call(
        finish_kernel,
        out_shape=(jax.ShapeDtypeStruct((part, n), jnp.float32), jax.ShapeDtypeStruct(front.shape, jnp.float32)),
        grid_spec=pltpu.PrefetchScalarGridSpec(
            num_scalar_prefetch=1,
            grid=(),
            in_specs=[vmem] * 6,
            out_specs=(vmem, vmem),
            scratch_shapes=[pltpu.VMEM((n, n), jnp.float32), pltpu.VMEM((n, n), jnp.float32)],
        ),
        compiler_params=pltpu.CompilerParams(vmem_limit_bytes=24 << 20),
        cost_estimate=pl.CostEstimate(flops=0, bytes_accessed=0, transcendentals=0),
        name="finish",
    )(mask, got, place.reshape(1, n), mine, other, front, near)


def share_panel(panel):
    count = lax.axis_size("col")
    around = count // 2
    half = panel.shape[0] // 2

    def turn(value, by):
        return lax.ppermute(value, "col", [(c, (c // 2 + by) % around * 2 + c % 2) for c in range(count)])

    before, after = turn(panel, 1), turn(panel, -1)
    far_low, far_high = turn(before[:half], 1), turn(after[half:], -1)
    mine = jnp.concatenate([panel, after, far_low, far_high, before])
    return mine, lax.ppermute(mine, "col", [(c, c ^ 1) for c in range(count)])


def body(front, contrib, target, mask, panel, pivots):
    row_count = lax.axis_size("row")
    col_count = lax.axis_size("col")
    row_index = lax.axis_index("row")
    col_index = lax.axis_index("col")
    layer = row_index // PLANE
    tile_rows, tile_cols = front.shape
    blocks_own = tile_rows // BLK
    sent_count = contrib.shape[0] // BLK
    width = pivots.shape[0]
    planes = [[z * PLANE + i for i in range(PLANE)] for z in range(LAYERS)]

    pillars = [[z * PLANE + i for z in range(LAYERS)] for i in range(PLANE)]

    def exchange(value, groups_of):
        return lax.all_to_all(
            value, "row", split_axis=0, concat_axis=0, axis_index_groups=groups_of, tiled=True
        )

    def over_plane(value):
        return exchange(value, planes)

    def over_z(value):
        return exchange(value, pillars)

    def along_z(value, away):
        return lax.ppermute(value, "row", [(r, r ^ (away * PLANE)) for r in range(row_count)])

    rank = jnp.sum((pivots[:, None] > pivots[None, :]).astype(jnp.int32), axis=1)
    groups = row_index ^ (jnp.arange(LAYERS, dtype=jnp.int32) * PLANE)
    slots = (groups[:, None] * PICK + jnp.arange(PICK, dtype=jnp.int32)[None, :]).reshape(-1)
    chosen = jnp.sum(jnp.where(rank[None, :] == slots[:, None], pivots[None, :], 0), axis=1)
    offsets = chosen - jnp.repeat(groups, PICK) * tile_rows

    plane_targets = lax.dynamic_slice_in_dim(target.reshape(row_count, sent_count), layer * PLANE, PLANE, 0)
    hit = (plane_targets // blocks_own)[:, None, :] == groups[None, :, None]
    kinds = jnp.sum(jnp.where(hit, (plane_targets % blocks_own + 1)[:, None, :], 0), axis=2).reshape(-1) - 1

    arrived = over_plane(pack(target, contrib.reshape(sent_count, BLK, tile_cols)))
    panel_rows = panel.shape[0]
    mine, other = share_panel(panel)
    owner, around = offsets[:PICK] // panel_rows, col_count // 2
    turns = (owner // 2 - col_index // 2) % around
    across = (owner + col_index) % 2
    spots = (across * around + turns) * panel_rows + offsets[:PICK] % panel_rows
    picker = (offsets[:PICK, None] == jnp.arange(tile_rows, dtype=jnp.int32)[None, :]).astype(jnp.float32)
    front_picked = exact_dot(picker, front)
    place = (rank // PICK) % PLANE * (LAYERS * PICK) + rank // (PICK * PLANE) * PICK + rank % PICK
    arrived, place = lax.optimization_barrier((arrived, place))

    near0, near1, far2, far3, lines = fold(kinds, offsets, spots, arrived, front_picked, mine, other)
    spread = over_z(jnp.broadcast_to(lines[None], (LAYERS,) + lines.shape))
    lines = jnp.sum(spread[:, : LAYERS * PICK], axis=0)
    lines, near1, far2, far3 = lax.optimization_barrier((lines, near1, far2, far3))
    got1, got2, got3 = along_z(near1, 1), along_z(far2, 2), along_z(far3, 3)
    got = over_plane(jnp.broadcast_to(lines[None], (PLANE,) + lines.shape))
    lower_own, kept = finish(mask.reshape(-1), got, place, mine, other, front, near0, panel_rows)
    return (lower_own, decode(kept, spread, (got1, got2, got3)))


def solution(mesh):
    placed = (P("row", "col"), P("row", "col"), P(), P("row", "col"), P(("row", "col"), None), P())
    return jax.shard_map(
        body,
        mesh=mesh,
        in_specs=placed,
        out_specs=(P(("row", "col"), None), P("row", "col")),
        check_vma=False,
    )
```
